256 devices in a mesh: energy: 8 (over x, z_hi), strip: 32 (over y, z_lo, core).
Axes of the slice: x: 4, y: 4, z: 8 (z_hi: 2, z_lo: 4; z = z_hi * 4 + z_lo), core: 2. Of those that a mesh axis runs over, the one named last changes fastest.
Arguments:
- object_field: float32 [64, 2, 2048, 384], P('energy', None, 'strip'), may hold values from -5 to 5
- probe_modes: float32 [64, 3, 2, 128, 128], P('energy'), may hold values from -2.5 to 2.5
- measured: float32 [64, 32, 5, 128, 128], P('energy', 'strip'), may hold values from 0.5 to 3
- scan_cols: int32 [32, 5], replicated, may hold values from 0 to 256, as said below
- spectra: float32 [64, 2, 8], replicated, may hold values from -4 to 4
- material_order: int32 [8], replicated, may hold values from 0 to 7, each once
Outputs:
- refined_object: float32 [64, 2, 2048, 384], P('energy', None, 'strip')
- abundance: float32 [8, 2, 32, 64, 384], P(None, None, 'strip', 'energy')
The draws below stay inside these ranges and needn't reach their ends.
Inputs may be any that keep to these rules, and one draw needn't show every extreme that they name: `scan_cols`: row b lists the first columns of the scan positions of band b, whose top row is b * 64; they rise, neighbours differ by 32 to 96, the first is 0 and the last 256. `material_order`: each material once.
All inputs are finite; a program needn't handle non-finite values.
Results may differ from the reference program's by a relative error of at most 0.0013.
Values sent between devices are 32-bit elements; how exact they have to be, the bound alone decides.
No kernel may reach another device: no remote copies, remote signals or barrier semaphores. Data moves between devices by JAX's collectives and lax.ppermute only.
A program may use at most 64 MiB of HBM per device.

```python
import jax
import jax.numpy as jnp
from jax import lax

PSIZE = 128
MODES = 3
MATS = 8
ENERGIES = 64
STEP = 64
COLS = 384
OUTER = 1
INNER = 1
BANDS = 32
ROWS = 2048
POS = 5


def draw_scan_cols(key, part):
    base_cols = jnp.arange(POS, dtype=jnp.int32) * STEP
    jitter = jax.random.randint(jax.random.fold_in(key, 11), (BANDS, POS), -(STEP // 4), STEP // 4 + 1, dtype=jnp.int32)
    offsets = jnp.clip(base_cols[None, :] + jitter, 0, COLS - PSIZE)
    offsets = offsets.at[:, 0].set(0)
    offsets = offsets.at[:, POS - 1].set(COLS - PSIZE)
    return offsets.astype(jnp.int32)


def levels(rng, shape, cuts, least, largest):
    def one(dim, parts):
        steps = jax.random.uniform(jax.random.fold_in(jax.random.fold_in(rng, 6), dim), (parts,), jnp.float32, least / len(cuts), largest / len(cuts))
        return jnp.repeat(jnp.exp(steps), shape[dim] // parts).reshape((-1,) + (1,) * (len(shape) - dim - 1))

    level = one(*cuts[0])
    for cut in cuts[1:]:
        level = level * one(*cut)
    return level


def normal_values(stream_key, shape, width, reach, shards=(), held_as=jnp.bfloat16):
    factor_of = levels(stream_key, shape, shards, -0.22, 0.18) if shards else 1.0
    entries = jax.random.normal(stream_key, shape, jnp.float32) * width * factor_of
    return jnp.minimum(jnp.maximum(entries, -reach), reach).astype(held_as)


def setup_inputs(seed: int = 0) -> dict:
    splits = jax.random.split(jax.random.key(seed), 7)
    return {
        "object_field": normal_values(splits[0], (ENERGIES, 2, ROWS, COLS), 1.0, 5.0, ((0, 8), (2, 32)), jnp.float32),
        "probe_modes": normal_values(splits[1], (ENERGIES, MODES, 2, PSIZE, PSIZE), 0.5, 2.5, ((0, 8),), jnp.float32),
        "measured": jnp.clip(0.5 + 2.5 * jax.random.uniform(splits[2], (ENERGIES, BANDS, POS, PSIZE, PSIZE), jnp.float32) ** levels(splits[2], (ENERGIES, BANDS, POS, PSIZE, PSIZE), ((0, 8), (1, 32)), -0.2, 0.2), 0.5, 3.0),
        "scan_cols": draw_scan_cols(jax.random.fold_in(splits[6], 71), 0),
        "spectra": normal_values(splits[4], (ENERGIES, 2, MATS), 1.0, 4.0, (), jnp.float32),
        "material_order": jax.random.permutation(splits[5], MATS).astype(jnp.int32),
    }


PRECISE = lax.Precision.HIGHEST

def dft_tables(probe_width, phase_sign):
    counter = jnp.arange(probe_width, dtype=jnp.int32)
    phase_index = counter[:, None] * counter[None, :] % probe_width
    angle_grid = phase_index.astype(jnp.float32) * (2.0 * jnp.pi / probe_width)
    root_width = jnp.sqrt(jnp.float32(probe_width))
    cosine_table = (jnp.cos(angle_grid) / root_width).astype(jnp.bfloat16)
    sine_table = (phase_sign * jnp.sin(angle_grid) / root_width).astype(jnp.bfloat16)
    blocks = jnp.stack([jnp.stack([cosine_table, sine_table]), jnp.stack([-sine_table, cosine_table])])
    return (blocks.transpose(0, 2, 1, 3), blocks.transpose(1, 2, 0, 3))

def transform(left_table, right_table, waves):
    first_section = jnp.einsum('dacj,emcjb->emdab', left_table.astype(jnp.float32), waves.astype(jnp.float32), precision=PRECISE)
    first_section = lax.optimization_barrier(first_section.astype(jnp.bfloat16))
    return jnp.einsum('emcab,cbdk->emdak', first_section.astype(jnp.float32), right_table.astype(jnp.float32), precision=PRECISE)

def band_gradient(window, measured_band, band_cols, probe_modes, tables):
    forward_left, forward_right, inverse_left, inverse_right = tables
    probe_real = probe_modes[:, :, 0]
    probe_imag = probe_modes[:, :, 1]

    def accumulate(position, gradient_total):
        column = lax.dynamic_index_in_dim(band_cols, position, 0, keepdims=False)
        measured_point = lax.dynamic_index_in_dim(measured_band, position, 1, keepdims=False)
        object_patch = lax.dynamic_slice_in_dim(window, column, PSIZE, axis=3)
        object_real = object_patch[:, None, 0]
        object_imag = object_patch[:, None, 1]
        exit_wave = jnp.stack([probe_real * object_real - probe_imag * object_imag, probe_real * object_imag + probe_imag * object_real], axis=2)
        exit_wave = lax.optimization_barrier(exit_wave.astype(jnp.bfloat16))
        spectrum = transform(forward_left, forward_right, exit_wave)
        intensity = lax.optimization_barrier(jnp.sum(spectrum * spectrum, axis=(1, 2)))
        scaling = measured_point / jnp.sqrt(jnp.maximum(intensity, 0.25))
        corrected = lax.optimization_barrier((spectrum * scaling[:, None, None]).astype(jnp.bfloat16))
        returned = transform(inverse_left, inverse_right, corrected)
        residual_wave = exit_wave.astype(jnp.float32) - returned
        wave_real = residual_wave[:, :, 0]
        wave_imag = residual_wave[:, :, 1]
        grad_real = lax.optimization_barrier(jnp.sum(probe_real * wave_real + probe_imag * wave_imag, axis=1))
        grad_imag = lax.optimization_barrier(jnp.sum(probe_real * wave_imag - probe_imag * wave_real, axis=1))
        update = jnp.stack([grad_real, grad_imag], axis=1)
        current = lax.dynamic_slice_in_dim(gradient_total, column, PSIZE, axis=3)
        return lax.dynamic_update_slice_in_dim(gradient_total, current + update, column, axis=3)
    return lax.fori_loop(0, POS, accumulate, jnp.zeros_like(window))

def descent_pass(estimate, measured, scan_cols, probe_modes, tables, step_size):
    padded = jnp.pad(estimate, ((0, 0), (0, 0), (0, STEP), (0, 0)))

    def band_step(gradient_sum, band_index):
        first_row = band_index * STEP
        window = lax.dynamic_slice_in_dim(padded, first_row, PSIZE, axis=2)
        measured_band = lax.dynamic_index_in_dim(measured, band_index, 1, keepdims=False)
        band_cols = lax.dynamic_index_in_dim(scan_cols, band_index, 0, keepdims=False)
        gradient = band_gradient(window, measured_band, band_cols, probe_modes, tables)
        current = lax.dynamic_slice_in_dim(gradient_sum, first_row, PSIZE, axis=2)
        return (lax.dynamic_update_slice_in_dim(gradient_sum, current + gradient, first_row, axis=2), None)
    gradient_sum, _ = lax.scan(band_step, jnp.zeros_like(padded), jnp.arange(BANDS, dtype=jnp.int32))
    return estimate - step_size[:, None, None, None] * gradient_sum[:, :, :ROWS]

def build_basis(spectra):
    spectra_real = spectra[:, 0]
    spectra_imag = spectra[:, 1]
    upper_rows = jnp.stack([spectra_real, -spectra_imag], axis=-1)
    lower_rows = jnp.stack([spectra_imag, spectra_real], axis=-1)
    return jnp.stack([upper_rows, lower_rows], axis=1).reshape(2 * ENERGIES, 2 * MATS)

def reference(object_field, probe_modes, measured, scan_cols, spectra, material_order):
    forward_left, forward_right = dft_tables(PSIZE, 1)
    inverse_left, inverse_right = dft_tables(PSIZE, -1)
    tables = (forward_left, forward_right, inverse_left, inverse_right)
    probe_power = lax.optimization_barrier(jnp.sum(probe_modes * probe_modes, axis=(1, 2)))
    step_size = 0.5 / lax.optimization_barrier(jnp.max(probe_power, axis=(1, 2)))
    basis_matrix = build_basis(spectra)
    gram_matrix = jnp.dot(basis_matrix.T, basis_matrix, precision=PRECISE)
    solver_map = jnp.linalg.solve(gram_matrix, basis_matrix.T)
    estimate = object_field
    coefficients = jnp.zeros((2 * MATS, ROWS * COLS), jnp.float32)
    for outer_step in range(OUTER):
        for inner_step in range(INNER):
            estimate = descent_pass(estimate, measured, scan_cols, probe_modes, tables, step_size)
        spectra_rows = estimate.reshape(2 * ENERGIES, ROWS * COLS)
        coefficients = jnp.dot(solver_map, spectra_rows, precision=PRECISE)
        estimate = jnp.dot(basis_matrix, coefficients, precision=PRECISE).reshape(ENERGIES, 2, ROWS, COLS)
    abundance = coefficients.reshape(MATS, 2, BANDS, STEP, COLS)
    abundance = jnp.take(abundance, material_order, axis=0)
    return (estimate, abundance)
```

```python
import functools

import jax
import jax.numpy as jnp
import numpy as np
from jax import lax
from jax.experimental import pallas as pl
from jax.experimental.pallas import tpu as pltpu
from jax.sharding import PartitionSpec as P

PRECISE = lax.Precision.HIGHEST
LANES = 128


def shifted(block, axis, distance):
    devices = range(lax.axis_size(axis))
    route = [(i - distance, i) for i in devices if i - distance in devices]
    return lax.ppermute(block, axis, route)


def dft_tables(width):
    counter = np.arange(width)
    angle = 2.0 * np.pi * (counter[:, None] * counter[None, :] % width) / width
    cosine = (np.cos(angle) / np.sqrt(width)).astype(np.float32)
    sine = (np.sin(angle) / np.sqrt(width)).astype(np.float32)
    left = np.block([[cosine, sine], [-sine, cosine]])
    right = np.block([[cosine, -sine], [sine, cosine]])
    return jnp.asarray(left).astype(jnp.bfloat16), jnp.asarray(right).astype(jnp.bfloat16)


def transform(left, right, waves):
    width = waves[0][0].shape[0]
    stacked = jnp.concatenate([jnp.concatenate(pair, axis=0) for pair in waves], axis=1)
    half = jnp.dot(left, stacked, preferred_element_type=jnp.float32).astype(jnp.bfloat16)
    rows = []
    for m in range(len(waves)):
        cols = slice(m * width, (m + 1) * width)
        rows.append(jnp.concatenate([half[:width, cols], half[width:, cols]], axis=1))
    full = jnp.dot(
        jnp.concatenate(rows, axis=0), right, preferred_element_type=jnp.float32
    )
    return [
        (full[m * width:(m + 1) * width, :width], full[m * width:(m + 1) * width, width:])
        for m in range(len(waves))
    ]


def gradient_kernel(
    cols_ref, left_ref, right_ref, top_ref, low_ref, probe_ref, measured_ref,
    own_ref, carried_ref, total,
):
    modes = probe_ref.shape[1]
    width = probe_ref.shape[-1]
    half = width // 2
    positions = measured_ref.shape[1]
    blocks = total.shape[-1] // LANES
    left = left_ref[...]
    right = right_ref[...]
    lane = lax.broadcasted_iota(jnp.int32, (width, width), 1)
    power = jnp.zeros((width, width), jnp.float32)
    for m in range(modes):
        power += probe_ref[0, m, 0] * probe_ref[0, m, 0] + probe_ref[0, m, 1] * probe_ref[0, m, 1]
    peak = jnp.max(jnp.max(power, axis=0, keepdims=True), axis=1, keepdims=True)
    step = 0.5 / peak
    total[...] = jnp.zeros_like(total)

    def window(part, start):
        cols = pl.ds(pl.multiple_of(start, LANES), LANES)
        return jnp.concatenate([top_ref[0, part, :, cols], low_ref[0, part, :, cols]], axis=0)

    for p in range(positions):
        column = cols_ref[p]
        first = column // LANES * LANES
        second = jnp.minimum(first + LANES, (blocks - 1) * LANES)
        offset = column - first
        back = lax.rem(LANES - offset, LANES)
        patch = []
        for part in range(2):
            here = pltpu.roll(window(part, first), back, 1)
            there = pltpu.roll(window(part, second), back, 1)
            patch.append(jnp.where(lane < LANES - offset, here, there))
        waves = []
        for m in range(modes):
            pr, pi = probe_ref[0, m, 0], probe_ref[0, m, 1]
            waves.append((
                (pr * patch[0] - pi * patch[1]).astype(jnp.bfloat16),
                (pr * patch[1] + pi * patch[0]).astype(jnp.bfloat16),
            ))
        spectrum = transform(left, right, waves)
        intensity = sum(r * r + i * i for r, i in spectrum)
        scale = measured_ref[0, p] * lax.rsqrt(jnp.maximum(intensity, 0.25))
        flipped = -scale
        corrected = [
            ((r * scale).astype(jnp.bfloat16), (i * flipped).astype(jnp.bfloat16))
            for r, i in spectrum
        ]
        returned = transform(left, right, corrected)
        grad_real = grad_imag = None
        for m in range(modes):
            pr, pi = probe_ref[0, m, 0], probe_ref[0, m, 1]
            wr = waves[m][0].astype(jnp.float32) - returned[m][0]
            wi = waves[m][1].astype(jnp.float32) + returned[m][1]
            gr = pr * wr + pi * wi
            gi = pr * wi - pi * wr
            grad_real = gr if m == 0 else grad_real + gr
            grad_imag = gi if m == 0 else grad_imag + gi
        for part, grad in enumerate((grad_real, grad_imag)):
            moved = pltpu.roll(grad, offset, 1)
            here = pl.ds(pl.multiple_of(first, LANES), LANES)
            there = pl.ds(pl.multiple_of(second, LANES), LANES)
            total[part, :, here] += jnp.where(lane >= offset, moved, 0.0)
            total[part, :, there] += jnp.where(lane < offset, moved, 0.0)
    own_ref[0] = top_ref[0] - step * total[:, :half]
    carried_ref[0] = step * total[:, half:]


def band_update(own_cols, left, right, top, low, probe, measured):
    energies, parts, rows, cols = top.shape
    _, modes, _, width, _ = probe.shape
    positions = measured.shape[1]
    band = pl.BlockSpec((1, parts, rows, cols), lambda e: (e, 0, 0, 0))
    table = pl.BlockSpec(left.shape, lambda e: (0, 0))
    return pl.pallas_call(
        gradient_kernel,
        grid=(energies,),
        in_specs=[
            pl.BlockSpec(memory_space=pltpu.SMEM),
            table,
            table,
            band,
            band,
            pl.BlockSpec((1, modes, parts, width, width), lambda e: (e, 0, 0, 0, 0)),
            pl.BlockSpec((1, positions, width, width), lambda e: (e, 0, 0, 0)),
        ],
        out_specs=[band, band],
        out_shape=[jax.ShapeDtypeStruct(top.shape, jnp.float32)] * 2,
        scratch_shapes=[pltpu.VMEM((parts, width, cols), jnp.float32)],
        name="band_update",
    )(own_cols, left, right, top, low, probe, measured)


def build_basis(spectra):
    spectra_real = spectra[:, 0]
    spectra_imag = spectra[:, 1]
    upper_rows = jnp.stack([spectra_real, -spectra_imag], axis=-1)
    lower_rows = jnp.stack([spectra_imag, spectra_real], axis=-1)
    stacked = jnp.stack([upper_rows, lower_rows], axis=1)
    return stacked.reshape(2 * spectra.shape[0], 2 * spectra.shape[2])


def on_device(object_field, probe_modes, measured, scan_cols, spectra, material_order):
    left, right = dft_tables(probe_modes.shape[-1])
    basis_matrix = build_basis(spectra)
    gram_matrix = jnp.dot(basis_matrix.T, basis_matrix, precision=PRECISE)
    factor = jnp.linalg.cholesky(gram_matrix)
    solver_map = jax.scipy.linalg.cho_solve((factor, True), basis_matrix.T)
    materials = spectra.shape[2]
    col_count = object_field.shape[3]
    strip_index = lax.axis_index("strip")
    own_cols = lax.dynamic_index_in_dim(scan_cols, strip_index, 0, keepdims=False)
    lower_rows = shifted(object_field, "strip", -1)
    own, carried = band_update(
        own_cols, left, right, object_field, lower_rows, probe_modes, measured[:, 0]
    )
    estimate = own - shifted(carried, "strip", 1)
    gathered = lax.all_to_all(estimate, "energy", split_axis=2, concat_axis=0, tiled=True)
    sub_rows = gathered.shape[2]
    spectra_rows = gathered.reshape(2 * gathered.shape[0], sub_rows * col_count)
    coefficients = jnp.dot(solver_map, spectra_rows, precision=PRECISE)
    projected = jnp.dot(basis_matrix, coefficients, precision=PRECISE).reshape(gathered.shape)
    estimate = lax.all_to_all(projected, "energy", split_axis=0, concat_axis=2, tiled=True)
    abundance = coefficients.reshape(materials, 2, 1, sub_rows, col_count)
    abundance = jnp.take(abundance, material_order, axis=0)
    return (estimate, abundance)


def solution(mesh):
    return jax.shard_map(
        on_device,
        mesh=mesh,
        in_specs=(
            P("energy", None, "strip", None),
            P("energy", None, None, None, None),
            P("energy", "strip", None, None, None),
            P(),
            P(),
            P(),
        ),
        out_specs=(P("energy", None, "strip", None), P(None, None, "strip", "energy", None)),
        check_vma=False,
    )
```

```python
import functools

import jax
import jax.numpy as jnp
import numpy as np
from jax import lax
from jax.experimental import pallas as pl
from jax.experimental.pallas import tpu as pltpu
from jax.sharding import PartitionSpec as P

PRECISE = lax.Precision.HIGHEST
LANES = 128
SUBLANES = 8
GROUP = 2
CHUNK = 4


def shifted(block, axis, distance):
    devices = range(lax.axis_size(axis))
    route = [(i - distance, i) for i in devices if i - distance in devices]
    return lax.ppermute(block, axis, route)


def dft_tables(width):
    counter = np.arange(width)
    angle = 2.0 * np.pi * (counter[:, None] * counter[None, :] % width) / width
    cosine = (np.cos(angle) / np.sqrt(width)).astype(np.float32)
    sine = (np.sin(angle) / np.sqrt(width)).astype(np.float32)
    left = np.block([[cosine, sine], [-sine, cosine]])
    right = np.block([[cosine, -sine], [sine, cosine]])
    return jnp.asarray(left).astype(jnp.bfloat16), jnp.asarray(right).astype(jnp.bfloat16)


def transform(left, right, waves):
    width = waves[0][0].shape[0]
    stacked = jnp.concatenate([jnp.concatenate(pair, axis=0) for pair in waves], axis=1)
    half = jnp.dot(left, stacked, preferred_element_type=jnp.float32).astype(jnp.bfloat16)
    rows = []
    for m in range(len(waves)):
        cols = slice(m * width, (m + 1) * width)
        rows.append(jnp.concatenate([half[:width, cols], half[width:, cols]], axis=1))
    full = jnp.dot(
        jnp.concatenate(rows, axis=0), right, preferred_element_type=jnp.float32
    )
    return [
        (full[m * width:(m + 1) * width, :width], full[m * width:(m + 1) * width, width:])
        for m in range(len(waves))
    ]


def gradient_kernel(
    cols_ref, left_ref, right_ref, top_ref, low_ref, probe_ref, measured_ref,
    own_ref, carried_ref, total,
):
    energies, modes = probe_ref.shape[:2]
    width = probe_ref.shape[-1]
    half = width // 2
    left, right = left_ref[...], right_ref[...]
    lane = lax.broadcasted_iota(jnp.int32, (width, width), 1)
    power = [
        sum(probe_ref[e, m, q] * probe_ref[e, m, q] for m in range(modes) for q in range(2))
        for e in range(energies)
    ]
    step = [
        0.5 / jnp.max(jnp.max(p, axis=0, keepdims=True), axis=1, keepdims=True) for p in power
    ]

    def window(e, part, start):
        cols = pl.ds(start, LANES)
        return jnp.concatenate([top_ref[e, part, :, cols], low_ref[e, part, :, cols]], axis=0)

    bases = [0, 0, pl.multiple_of(cols_ref[2] // LANES * LANES, LANES), LANES, 2 * LANES]
    moves = [None, cols_ref[1], cols_ref[2] - bases[2], cols_ref[3] - LANES, None]

    def patch_of(e, p):
        base, offset = bases[p], moves[p]
        if offset is None:
            return [window(e, part, base) for part in range(2)]
        back = lax.rem(LANES - offset, LANES)
        patch = []
        for part in range(2):
            here = pltpu.roll(window(e, part, base), back, 1)
            there = pltpu.roll(window(e, part, base + LANES), back, 1)
            patch.append(jnp.where(lane < LANES - offset, here, there))
        return patch

    def add(e, part, start, value):
        at = pl.ds(start, LANES)
        total[e, part, :, at] += value

    for e in range(energies):
        total[e] = jnp.zeros(total.shape[1:], jnp.float32)
    for p in range(5):
        patches = [patch_of(e, p) for e in range(energies)]
        waves = []
        for e in range(energies):
            real, imag = patches[e]
            for m in range(modes):
                pr, pi = probe_ref[e, m, 0], probe_ref[e, m, 1]
                waves.append((
                    (pr * real - pi * imag).astype(jnp.bfloat16),
                    (pr * imag + pi * real).astype(jnp.bfloat16),
                ))
        spectrum = transform(left, right, waves)
        corrected = []
        for e in range(energies):
            mine = spectrum[e * modes:(e + 1) * modes]
            intensity = sum(r * r + i * i for r, i in mine)
            scale = measured_ref[e, p] * lax.rsqrt(jnp.maximum(intensity, 0.25))
            flipped = -scale
            corrected += [
                ((r * scale).astype(jnp.bfloat16), (i * flipped).astype(jnp.bfloat16))
                for r, i in mine
            ]
        returned = transform(left, right, corrected)
        for e in range(energies):
            patch = patch_of(e, p)
            grads = [power[e] * patch[0], power[e] * patch[1]]
            for m in range(modes):
                pr, pi = probe_ref[e, m, 0], probe_ref[e, m, 1]
                rr, ri = returned[e * modes + m]
                grads[0] -= pr * rr - pi * ri
                grads[1] += pr * ri + pi * rr
            for part, grad in enumerate(grads):
                if moves[p] is None:
                    add(e, part, bases[p], grad)
                else:
                    moved = pltpu.roll(grad, moves[p], 1)
                    add(e, part, bases[p], jnp.where(lane >= moves[p], moved, 0.0))
                    add(e, part, bases[p] + LANES, jnp.where(lane < moves[p], moved, 0.0))
    for e in range(energies):
        own_ref[e] = top_ref[e] - step[e] * total[e, :, :half]
        carried_ref[e] = step[e] * total[e, :, half:]


def band_update(chunk, own_cols, left, right, top, low, probe, measured):
    _, parts, rows, cols = top.shape
    _, modes, _, width, _ = probe.shape
    positions = measured.shape[1]
    start = chunk * CHUNK // GROUP
    band = pl.BlockSpec((GROUP, parts, rows, cols), lambda e: (e, 0, 0, 0))
    table = pl.BlockSpec(left.shape, lambda e: (0, 0))
    pairs = CHUNK * positions
    return pl.pallas_call(
        gradient_kernel,
        grid=(CHUNK // GROUP,),
        in_specs=[
            pl.BlockSpec(memory_space=pltpu.SMEM),
            table,
            table,
            pl.BlockSpec((GROUP, parts, rows, cols), lambda e: (e + start, 0, 0, 0)),
            band,
            pl.BlockSpec((GROUP, modes, parts, width, width), lambda e: (e + start, 0, 0, 0, 0)),
            pl.BlockSpec((GROUP, positions, width, width), lambda e: (e + start, 0, 0, 0)),
        ],
        out_specs=[band, band],
        out_shape=[jax.ShapeDtypeStruct((CHUNK, parts, rows, cols), jnp.float32)] * 2,
        scratch_shapes=[pltpu.VMEM((GROUP, parts, width, cols), jnp.float32)],
        cost_estimate=pl.CostEstimate(
            flops=pairs * 500_000_000, bytes_accessed=pairs * 200_000, transcendentals=0
        ),
        name="band_update",
    )(own_cols, left, right, top, low, probe, measured)


def project_kernel(place_ref, weight_ref, *refs):
    chunks = 2
    owns, received, outs = refs[:chunks], refs[chunks:2 * chunks], refs[2 * chunks:]
    energies, parts = owns[0].shape[:2]
    slots = len(outs) // 2
    weight = weight_ref[...]
    for h in range(2):
        for d in range(slots):
            start = (lax.rem(place_ref[0] + d, slots) * 2 + h) * SUBLANES
            at = pl.ds(pl.multiple_of(start, SUBLANES), SUBLANES)
            values = [
                own[e, q, at] - got[e, q, at]
                for own, got in zip(owns, received) for e in range(energies) for q in range(parts)
            ]
            outs[h * slots + d][...] = jnp.dot(
                weight, jnp.concatenate(values, axis=0),
                precision=PRECISE, preferred_element_type=jnp.float32,
            )


def project(place, weight, owns, received):
    slots = 4
    smem = pl.BlockSpec(memory_space=pltpu.SMEM)
    vmem = pl.BlockSpec(memory_space=pltpu.VMEM)
    out = jax.ShapeDtypeStruct((weight.shape[0], owns[0].shape[-1]), jnp.float32)
    return pl.pallas_call(
        project_kernel,
        in_specs=[smem] + [vmem] * (1 + len(owns) + len(received)),
        out_specs=[vmem] * (2 * slots),
        out_shape=[out] * (2 * slots),
        cost_estimate=pl.CostEstimate(flops=800_000_000, bytes_accessed=4_000_000, transcendentals=0),
        name="project",
    )(place, weight, *owns, *received)


def expand_kernel(place_ref, weight_ref, *refs):
    slots = 4
    pieces, refined_ref = refs[:slots], refs[-1]
    parts = refined_ref.shape[1]
    weight = weight_ref[...]
    for d, piece in enumerate(pieces):
        values = jnp.dot(
            weight, piece[...], precision=PRECISE, preferred_element_type=jnp.float32
        )
        at = lax.rem(place_ref[0] + slots - d, slots)
        for j in range(values.shape[0] // SUBLANES):
            refined_ref[j // parts, j % parts, at, 0] = values[j * SUBLANES:(j + 1) * SUBLANES]


def expand(half, place, weight, pieces, shape, previous):
    smem = pl.BlockSpec(memory_space=pltpu.SMEM)
    in_specs = [smem] + [pl.BlockSpec(a.shape, lambda i: (0, 0)) for a in (weight, *pieces)]
    aliases = {}
    if previous:
        aliases = {len(in_specs): 0}
        in_specs += [pl.BlockSpec(memory_space=pl.ANY)]
    return pl.pallas_call(
        expand_kernel,
        grid=(1,),
        in_specs=in_specs,
        out_specs=pl.BlockSpec(shape[:3] + (1,) + shape[4:], lambda i: (0, 0, 0, half, 0, 0)),
        out_shape=jax.ShapeDtypeStruct(shape, jnp.float32),
        input_output_aliases=aliases,
        cost_estimate=pl.CostEstimate(flops=400_000_000, bytes_accessed=2_000_000, transcendentals=0),
        name="expand",
    )(place, weight, *pieces, *previous)


def pick_kernel(place_ref, order_ref, first_ref, second_ref, out_ref):
    second = place_ref[1] == 1
    for m in range(out_ref.shape[0]):
        for q in range(out_ref.shape[1]):
            row = (order_ref[m] * out_ref.shape[1] + q) * SUBLANES
            at = pl.ds(pl.multiple_of(row, SUBLANES), SUBLANES)
            out_ref[m, q, 0] = jnp.where(second, second_ref[at], first_ref[at])


def pick(place, order, first, second, shape):
    smem = pl.BlockSpec(memory_space=pltpu.SMEM)
    vmem = pl.BlockSpec(memory_space=pltpu.VMEM)
    return pl.pallas_call(
        pick_kernel,
        in_specs=[smem, smem, vmem, vmem],
        out_specs=vmem,
        out_shape=jax.ShapeDtypeStruct(shape, jnp.float32),
        cost_estimate=pl.CostEstimate(flops=1_000_000, bytes_accessed=600_000, transcendentals=0),
        name="pick",
    )(place, order, first, second)


def build_basis(spectra):
    spectra_real = spectra[:, 0]
    spectra_imag = spectra[:, 1]
    upper_rows = jnp.stack([spectra_real, -spectra_imag], axis=-1)
    lower_rows = jnp.stack([spectra_imag, spectra_real], axis=-1)
    stacked = jnp.stack([upper_rows, lower_rows], axis=1)
    return stacked.reshape(2 * spectra.shape[0], 2 * spectra.shape[2])


def along_x(block, distance):
    return lax.ppermute(block, "energy", [(e, (e + 2 * distance) % 8) for e in range(8)])


def along_z(block):
    return lax.ppermute(block, "energy", [(e, e ^ 1) for e in range(8)])


def on_device(object_field, probe_modes, measured, scan_cols, spectra, material_order):
    energies, parts, rows, columns = object_field.shape
    materials = spectra.shape[2]
    left, right = dft_tables(probe_modes.shape[-1])
    measured = measured[:, 0]
    own_cols = lax.dynamic_index_in_dim(scan_cols, lax.axis_index("strip"), 0, keepdims=False)
    lows = [
        shifted(object_field[e:e + CHUNK], "strip", -1) for e in range(0, energies, CHUNK)
    ]
    energy = lax.axis_index("energy")
    place = jnp.stack([energy // 2, energy % 2]).astype(jnp.int32)
    basis_matrix = build_basis(spectra)
    gram_matrix = jnp.dot(basis_matrix.T, basis_matrix, precision=PRECISE)
    factor = jnp.linalg.cholesky(gram_matrix)
    basis_own = lax.dynamic_slice_in_dim(
        basis_matrix, energy * energies * parts, energies * parts, axis=0
    )
    solver_own = jax.scipy.linalg.cho_solve((factor, True), basis_own.T)
    eye = jnp.eye(SUBLANES, dtype=jnp.float32)
    spread_solver = jnp.kron(solver_own, eye)
    spread_basis = jnp.kron(basis_own, eye)

    owns, received = [], []
    for chunk, low in enumerate(lows):
        own, carried = band_update(
            chunk, own_cols, left, right, object_field, low, probe_modes, measured
        )
        owns.append(own)
        received.append(shifted(carried, "strip", 1))
    sums = project(place, spread_solver, owns, received)
    mine = []
    for h in range(2):
        own, *others = sums[4 * h:4 * h + 4]
        share = own
        for d, other in enumerate(others):
            share = share + along_x(other, d + 1)
        mine.append(share + along_z(share))
    abundance = pick(
        place, material_order, *mine, (materials, parts, 1, SUBLANES, columns)
    )
    refined = ()
    shape = (energies, parts, 4, 2, SUBLANES, columns)
    for h in range(2):
        pieces = [mine[h]] + [along_x(mine[h], d) for d in (1, 2, 3)]
        refined = (expand(h, place, spread_basis, pieces, shape, refined),)
    return refined[0].reshape(object_field.shape), abundance


def solution(mesh):
    return jax.shard_map(
        on_device,
        mesh=mesh,
        in_specs=(
            P("energy", None, "strip", None),
            P("energy", None, None, None, None),
            P("energy", "strip", None, None, None),
            P(),
            P(),
            P(),
        ),
        out_specs=(P("energy", None, "strip", None), P(None, None, "strip", "energy", None)),
        check_vma=False,
    )
```

```python
import jax
import jax.numpy as jnp
import numpy as np
from jax import lax
from jax.experimental import pallas as pl
from jax.experimental.pallas import tpu as pltpu
from jax.sharding import PartitionSpec as P


PRECISE = lax.Precision.HIGHEST
LANES = 128
SUBLANES = 8
GROUP = 2
CHUNKS = (2, 2, 4)


def shifted(block, axis, distance):
    devices = range(lax.axis_size(axis))
    route = [(i - distance, i) for i in devices if i - distance in devices]
    return lax.ppermute(block, axis, route)


def dft_tables(width):
    counter = np.arange(width)
    angle = 2.0 * np.pi * (counter[:, None] * counter[None, :] % width) / width
    cosine = (np.cos(angle) / np.sqrt(width)).astype(np.float32)
    sine = (np.sin(angle) / np.sqrt(width)).astype(np.float32)
    left = np.block([[cosine, sine], [-sine, cosine]])
    right = np.block([[cosine, -sine], [sine, cosine]])
    return jnp.asarray(left).astype(jnp.bfloat16), jnp.asarray(right).astype(jnp.bfloat16)


def transform(left, right, waves):
    width = waves[0][0].shape[0]
    stacked = jnp.concatenate([jnp.concatenate(pair, axis=0) for pair in waves], axis=1)
    half = jnp.dot(left, stacked, preferred_element_type=jnp.float32).astype(jnp.bfloat16)
    rows = []
    for m in range(len(waves)):
        cols = slice(m * width, (m + 1) * width)
        rows.append(jnp.concatenate([half[:width, cols], half[width:, cols]], axis=1))
    full = jnp.dot(
        jnp.concatenate(rows, axis=0), right, preferred_element_type=jnp.float32
    )
    return [
        (full[m * width:(m + 1) * width, :width], full[m * width:(m + 1) * width, width:])
        for m in range(len(waves))
    ]


def gradient_kernel(
    cols_ref, left_ref, right_ref, top_ref, low_ref, probe_ref, measured_ref,
    own_ref, carried_ref, total,
):
    energies, modes = probe_ref.shape[:2]
    width = probe_ref.shape[-1]
    half = width // 2
    left, right = left_ref[...], right_ref[...]
    lane = lax.broadcasted_iota(jnp.int32, (width, width), 1)
    power = [
        sum(probe_ref[e, m, q] * probe_ref[e, m, q] for m in range(modes) for q in range(2))
        for e in range(energies)
    ]
    step = [
        0.5 / jnp.max(jnp.max(p, axis=0, keepdims=True), axis=1, keepdims=True) for p in power
    ]

    def window(e, part, start):
        cols = pl.ds(start, LANES)
        return jnp.concatenate([top_ref[e, part, :, cols], low_ref[e, part, :, cols]], axis=0)

    bases = [0, 0, pl.multiple_of(cols_ref[2] // LANES * LANES, LANES), LANES, 2 * LANES]
    moves = [None, cols_ref[1], cols_ref[2] - bases[2], cols_ref[3] - LANES, None]

    def patch_of(e, p):
        base, offset = bases[p], moves[p]
        if offset is None:
            return [window(e, part, base) for part in range(2)]
        back = lax.rem(LANES - offset, LANES)
        patch = []
        for part in range(2):
            here = pltpu.roll(window(e, part, base), back, 1)
            there = pltpu.roll(window(e, part, base + LANES), back, 1)
            patch.append(jnp.where(lane < LANES - offset, here, there))
        return patch

    def add(e, part, start, value):
        at = pl.ds(start, LANES)
        total[e, part, :, at] += value

    def forward(p):
        waves, patches = [], [patch_of(e, p) for e in range(energies)]
        for e in range(energies):
            real, imag = patches[e]
            for m in range(modes):
                pr, pi = probe_ref[e, m, 0], probe_ref[e, m, 1]
                waves.append((
                    (pr * real - pi * imag).astype(jnp.bfloat16),
                    (pr * imag + pi * real).astype(jnp.bfloat16),
                ))
        return patches, transform(left, right, waves)

    def correction(p, spectrum):
        corrected = []
        for e in range(energies):
            mine = spectrum[e * modes:(e + 1) * modes]
            intensity = sum(r * r + i * i for r, i in mine)
            scale = measured_ref[e, p] * lax.rsqrt(jnp.maximum(intensity, 0.25))
            flipped = -scale
            corrected += [
                ((r * scale).astype(jnp.bfloat16), (i * flipped).astype(jnp.bfloat16))
                for r, i in mine
            ]
        return corrected

    def gather(p, patches, returned):
        for e in range(energies):
            patch = patches[e]
            grads = [power[e] * patch[0], power[e] * patch[1]]
            for m in range(modes):
                pr, pi = probe_ref[e, m, 0], probe_ref[e, m, 1]
                rr, ri = returned[e * modes + m]
                grads[0] -= pr * rr - pi * ri
                grads[1] += pr * ri + pi * rr
            for part, grad in enumerate(grads):
                if p == 0:
                    total[e, part, :, :LANES] = grad
                elif moves[p] is None:
                    add(e, part, bases[p], grad)
                else:
                    moved = pltpu.roll(grad, moves[p], 1)
                    add(e, part, bases[p], jnp.where(lane >= moves[p], moved, 0.0))
                    there = jnp.where(lane < moves[p], moved, 0.0)
                    if p == 1:
                        total[e, part, :, LANES:2 * LANES] = there
                        total[e, part, :, 2 * LANES:] = jnp.zeros((width, LANES), jnp.float32)
                    else:
                        add(e, part, bases[p] + LANES, there)

    patches, spectrum = forward(0)
    for p in range(5):
        corrected = correction(p, spectrum)
        ahead = forward(p + 1) if p < 4 else None
        returned = transform(left, right, corrected)
        gather(p, patches, returned)
        if ahead:
            patches, spectrum = ahead
    for e in range(energies):
        own_ref[e] = top_ref[e] - step[e] * total[e, :, :half]
        carried_ref[e] = step[e] * total[e, :, half:]


def band_update(first, count, own_cols, left, right, top, low, probe, measured):
    _, parts, rows, cols = top.shape
    _, modes, _, width, _ = probe.shape
    positions = measured.shape[1]
    start = first // GROUP
    band = pl.BlockSpec((GROUP, parts, rows, cols), lambda e: (e, 0, 0, 0))
    table = pl.BlockSpec(left.shape, lambda e: (0, 0))
    pairs = count * positions
    return pl.pallas_call(
        gradient_kernel,
        grid=(count // GROUP,),
        in_specs=[
            pl.BlockSpec(memory_space=pltpu.SMEM),
            table,
            table,
            pl.BlockSpec((GROUP, parts, rows, cols), lambda e: (e + start, 0, 0, 0)),
            band,
            pl.BlockSpec((GROUP, modes, parts, width, width), lambda e: (e + start, 0, 0, 0, 0)),
            pl.BlockSpec((GROUP, positions, width, width), lambda e: (e + start, 0, 0, 0)),
        ],
        out_specs=[band, band],
        out_shape=[jax.ShapeDtypeStruct((count, parts, rows, cols), jnp.float32)] * 2,
        scratch_shapes=[pltpu.VMEM((GROUP, parts, width, cols), jnp.float32)],
        cost_estimate=pl.CostEstimate(
            flops=pairs * 500_000_000, bytes_accessed=pairs * 200_000, transcendentals=0
        ),
        name="band_update",
    )(own_cols, left, right, top, low, probe, measured)


def spread(matrix):
    wide = jnp.kron(matrix, jnp.eye(SUBLANES, dtype=jnp.float32))
    high = lax.reduce_precision(wide, 8, 7)
    return jnp.concatenate(
        [jnp.concatenate([part, part], axis=1) for part in (high, wide - high)], axis=0
    ).astype(jnp.bfloat16)


def times(weight, values):
    high = values.astype(jnp.bfloat16)
    low = (values - high.astype(jnp.float32)).astype(jnp.bfloat16)
    products = jnp.dot(
        weight, jnp.concatenate([high, low], axis=0), preferred_element_type=jnp.float32
    )
    rows = products.shape[0] // 2
    return products[:rows] + products[rows:]


def project_kernel(place_ref, weight_ref, *refs):
    chunks = len(CHUNKS)
    owns, received, outs = refs[:chunks], refs[chunks:2 * chunks], refs[2 * chunks:]
    slots, columns = len(outs), outs[0].shape[1]
    weight = weight_ref[...]
    stacks = []
    for d in range(slots):
        at = lax.rem(place_ref[0] + d, slots)
        values = [
            own[e, q, at, 0] - got[e, q, at, 0]
            for own, got in zip(owns, received)
            for e in range(own.shape[0]) for q in range(own.shape[1])
        ]
        stacks.append(jnp.concatenate(values, axis=0))
    for d in range(0, slots, 2):
        products = times(weight, jnp.concatenate(stacks[d:d + 2], axis=1))
        outs[d][...] = products[:, :columns]
        outs[d + 1][...] = products[:, columns:]


def project(half, place, weight, owns, received):
    slots = 4
    _, parts, _, columns = owns[0].shape
    shape = (parts, slots, 2, SUBLANES, columns)
    arrays = [a.reshape(a.shape[:1] + shape) for a in (*owns, *received)]
    out = jax.ShapeDtypeStruct((weight.shape[0] // 2, columns), jnp.float32)
    return pl.pallas_call(
        project_kernel,
        grid=(columns // LANES,),
        in_specs=[
            pl.BlockSpec(memory_space=pltpu.SMEM), pl.BlockSpec(weight.shape, lambda i: (0, 0))
        ] + [
            pl.BlockSpec(
                (a.shape[0], parts, slots, 1, SUBLANES, LANES), lambda i: (0, 0, 0, half, 0, i)
            )
            for a in arrays
        ],
        out_specs=[pl.BlockSpec((out.shape[0], LANES), lambda i: (0, i))] * slots,
        out_shape=[out] * slots,
        cost_estimate=pl.CostEstimate(flops=400_000_000, bytes_accessed=2_000_000, transcendentals=0),
        name="project",
    )(place, weight, *arrays)


def expand_kernel(place_ref, weight_ref, *refs):
    slots = 4
    pieces, refined_ref = refs[:slots], refs[-1]
    parts, columns = refined_ref.shape[1], pieces[0].shape[1]
    weight = weight_ref[...]
    for d in range(0, slots, 2):
        values = times(
            weight, jnp.concatenate([piece[...] for piece in pieces[d:d + 2]], axis=1)
        )
        for n in range(2):
            at = lax.rem(place_ref[0] + slots - d - n, slots)
            for j in range(values.shape[0] // SUBLANES):
                refined_ref[j // parts, j % parts, at, 0] = values[
                    j * SUBLANES:(j + 1) * SUBLANES, n * columns:(n + 1) * columns
                ]


def expand(half, place, weight, pieces, shape, previous):
    smem = pl.BlockSpec(memory_space=pltpu.SMEM)
    in_specs = [smem, pl.BlockSpec(weight.shape, lambda i: (0, 0))]
    in_specs += [pl.BlockSpec((a.shape[0], LANES), lambda i: (0, i)) for a in pieces]
    aliases = {}
    if previous:
        aliases = {len(in_specs): 0}
        in_specs += [pl.BlockSpec(memory_space=pl.ANY)]
    return pl.pallas_call(
        expand_kernel,
        grid=(shape[-1] // LANES,),
        in_specs=in_specs,
        out_specs=pl.BlockSpec(
            shape[:3] + (1, SUBLANES, LANES), lambda i: (0, 0, 0, half, 0, i)
        ),
        out_shape=jax.ShapeDtypeStruct(shape, jnp.float32),
        input_output_aliases=aliases,
        cost_estimate=pl.CostEstimate(flops=400_000_000, bytes_accessed=2_000_000, transcendentals=0),
        name="expand",
    )(place, weight, *pieces, *previous)


def pick_kernel(place_ref, order_ref, first_ref, second_ref, out_ref):
    second = place_ref[1] == 1
    for m in range(out_ref.shape[0]):
        for q in range(out_ref.shape[1]):
            row = (order_ref[m] * out_ref.shape[1] + q) * SUBLANES
            at = pl.ds(pl.multiple_of(row, SUBLANES), SUBLANES)
            out_ref[m, q, 0] = jnp.where(second, second_ref[at], first_ref[at])


def pick(place, order, first, second, shape):
    smem = pl.BlockSpec(memory_space=pltpu.SMEM)
    vmem = pl.BlockSpec(memory_space=pltpu.VMEM)
    return pl.pallas_call(
        pick_kernel,
        in_specs=[smem, smem, vmem, vmem],
        out_specs=vmem,
        out_shape=jax.ShapeDtypeStruct(shape, jnp.float32),
        cost_estimate=pl.CostEstimate(flops=1_000_000, bytes_accessed=600_000, transcendentals=0),
        name="pick",
    )(place, order, first, second)


def build_basis(spectra):
    spectra_real = spectra[:, 0]
    spectra_imag = spectra[:, 1]
    upper_rows = jnp.stack([spectra_real, -spectra_imag], axis=-1)
    lower_rows = jnp.stack([spectra_imag, spectra_real], axis=-1)
    stacked = jnp.stack([upper_rows, lower_rows], axis=1)
    return stacked.reshape(2 * spectra.shape[0], 2 * spectra.shape[2])


def along_x(block, distance):
    return lax.ppermute(block, "energy", [(e, (e + 2 * distance) % 8) for e in range(8)])


def along_z(block):
    return lax.ppermute(block, "energy", [(e, e ^ 1) for e in range(8)])


def on_device(object_field, probe_modes, measured, scan_cols, spectra, material_order):
    energies, parts, _, columns = object_field.shape
    materials = spectra.shape[2]
    left, right = dft_tables(probe_modes.shape[-1])
    measured = measured[:, 0]
    own_cols = lax.dynamic_index_in_dim(scan_cols, lax.axis_index("strip"), 0, keepdims=False)
    source, lows, first = object_field, [], 0
    for count in CHUNKS:
        block = source[first:first + count]
        if first == 0:
            source, block = lax.optimization_barrier((source, block))
        lows.append(shifted(block, "strip", -1))
        first += count
    energy = lax.axis_index("energy")
    place = jnp.stack([energy // 2, energy % 2]).astype(jnp.int32)
    basis_matrix = build_basis(spectra)
    gram_matrix = jnp.dot(basis_matrix.T, basis_matrix, precision=PRECISE)
    factor = jnp.linalg.cholesky(gram_matrix)
    basis_own = lax.dynamic_slice_in_dim(
        basis_matrix, energy * energies * parts, energies * parts, axis=0
    )
    solver_own = jax.scipy.linalg.cho_solve((factor, True), basis_own.T)
    spread_solver, spread_basis = spread(solver_own), spread(basis_own)

    owns, received, first = [], [], 0
    for count, low in zip(CHUNKS, lows):
        own, carried = band_update(
            first, count, own_cols, left, right, object_field, low, probe_modes, measured
        )
        owns.append(own)
        received.append(shifted(carried, "strip", 1))
        first += count
    mine = []
    for h in range(2):
        share, *others = project(h, place, spread_solver, owns, received)
        arrived = [along_x(other, d + 1) for d, other in enumerate(others)]
        share = share + arrived[0] + arrived[1] + arrived[2]
        arrived = along_z(share)
        mine.append(share + arrived)
    abundance = pick(
        place, material_order, *mine, (materials, parts, 1, SUBLANES, columns)
    )
    refined = ()
    shape = (energies, parts, 4, 2, SUBLANES, columns)
    for h in range(2):
        pieces = [mine[h]] + [along_x(mine[h], d) for d in (1, 2, 3)]
        refined = (expand(h, place, spread_basis, pieces, shape, refined),)
    return refined[0].reshape(object_field.shape), abundance


def solution(mesh):
    return jax.shard_map(
        on_device,
        mesh=mesh,
        in_specs=(
            P("energy", None, "strip", None),
            P("energy", None, None, None, None),
            P("energy", "strip", None, None, None),
            P(),
            P(),
            P(),
        ),
        out_specs=(P("energy", None, "strip", None), P(None, None, "strip", "energy", None)),
        check_vma=False,
    )
```

```python
import jax
import jax.numpy as jnp
import numpy as np
from jax import lax
from jax.experimental import pallas as pl
from jax.experimental.pallas import tpu as pltpu
from jax.sharding import PartitionSpec as P


PRECISE = lax.Precision.HIGHEST
LANES = 128
SUBLANES = 8
GROUP = 2
CHUNK = 4


def shifted(block, axis, distance):
    devices = range(lax.axis_size(axis))
    route = [(i - distance, i) for i in devices if i - distance in devices]
    return lax.ppermute(block, axis, route)


def dft_tables(width):
    counter = np.arange(width)
    angle = 2.0 * np.pi * (counter[:, None] * counter[None, :] % width) / width
    cosine = (np.cos(angle) / np.sqrt(width)).astype(np.float32)
    sine = (np.sin(angle) / np.sqrt(width)).astype(np.float32)
    left = np.block([[cosine, sine], [-sine, cosine]])
    right = np.block([[cosine, -sine], [sine, cosine]])
    return jnp.asarray(left).astype(jnp.bfloat16), jnp.asarray(right).astype(jnp.bfloat16)


def transform(left, right, waves):
    width = waves[0][0].shape[0]
    stacked = jnp.concatenate([jnp.concatenate(pair, axis=0) for pair in waves], axis=1)
    half = jnp.dot(left, stacked, preferred_element_type=jnp.float32).astype(jnp.bfloat16)
    rows = []
    for m in range(len(waves)):
        cols = slice(m * width, (m + 1) * width)
        rows.append(jnp.concatenate([half[:width, cols], half[width:, cols]], axis=1))
    full = jnp.dot(
        jnp.concatenate(rows, axis=0), right, preferred_element_type=jnp.float32
    )
    return [
        (full[m * width:(m + 1) * width, :width], full[m * width:(m + 1) * width, width:])
        for m in range(len(waves))
    ]


def gradient_kernel(
    cols_ref, left_ref, right_ref, top_ref, low_ref, probe_ref, measured_ref,
    own_ref, carried_ref, total,
):
    energies, modes = probe_ref.shape[:2]
    width = probe_ref.shape[-1]
    half = width // 2
    left, right = left_ref[...], right_ref[...]
    lane = lax.broadcasted_iota(jnp.int32, (width, width), 1)
    power = [
        sum(probe_ref[e, m, q] * probe_ref[e, m, q] for m in range(modes) for q in range(2))
        for e in range(energies)
    ]
    step = [
        0.5 / jnp.max(jnp.max(p, axis=0, keepdims=True), axis=1, keepdims=True) for p in power
    ]

    def window(e, part, start):
        cols = pl.ds(start, LANES)
        return jnp.concatenate([top_ref[e, part, :, cols], low_ref[e, part, :, cols]], axis=0)

    bases = [0, 0, pl.multiple_of(cols_ref[2] // LANES * LANES, LANES), LANES, 2 * LANES]
    moves = [None, cols_ref[1], cols_ref[2] - bases[2], cols_ref[3] - LANES, None]

    def patch_of(e, p):
        base, offset = bases[p], moves[p]
        if offset is None:
            return [window(e, part, base) for part in range(2)]
        back = lax.rem(LANES - offset, LANES)
        patch = []
        for part in range(2):
            here = pltpu.roll(window(e, part, base), back, 1)
            there = pltpu.roll(window(e, part, base + LANES), back, 1)
            patch.append(jnp.where(lane < LANES - offset, here, there))
        return patch

    def add(e, part, start, value):
        at = pl.ds(start, LANES)
        total[e, part, :, at] += value

    def forward(p):
        waves, patches = [], [patch_of(e, p) for e in range(energies)]
        for e in range(energies):
            real, imag = patches[e]
            for m in range(modes):
                pr, pi = probe_ref[e, m, 0], probe_ref[e, m, 1]
                waves.append((
                    (pr * real - pi * imag).astype(jnp.bfloat16),
                    (pr * imag + pi * real).astype(jnp.bfloat16),
                ))
        return patches, transform(left, right, waves)

    def correction(p, spectrum):
        corrected = []
        for e in range(energies):
            mine = spectrum[e * modes:(e + 1) * modes]
            intensity = sum(r * r + i * i for r, i in mine)
            scale = measured_ref[e, p] * lax.rsqrt(jnp.maximum(intensity, 0.25))
            flipped = -scale
            corrected += [
                ((r * scale).astype(jnp.bfloat16), (i * flipped).astype(jnp.bfloat16))
                for r, i in mine
            ]
        return corrected

    def gather(p, patches, returned):
        for e in range(energies):
            patch = patches[e]
            grads = [power[e] * patch[0], power[e] * patch[1]]
            for m in range(modes):
                pr, pi = probe_ref[e, m, 0], probe_ref[e, m, 1]
                rr, ri = returned[e * modes + m]
                grads[0] -= pr * rr - pi * ri
                grads[1] += pr * ri + pi * rr
            for part, grad in enumerate(grads):
                if p == 0:
                    total[e, part, :, :LANES] = grad
                elif moves[p] is None:
                    add(e, part, bases[p], grad)
                else:
                    moved = pltpu.roll(grad, moves[p], 1)
                    add(e, part, bases[p], jnp.where(lane >= moves[p], moved, 0.0))
                    there = jnp.where(lane < moves[p], moved, 0.0)
                    if p == 1:
                        total[e, part, :, LANES:2 * LANES] = there
                        total[e, part, :, 2 * LANES:] = jnp.zeros((width, LANES), jnp.float32)
                    else:
                        add(e, part, bases[p] + LANES, there)

    patches, spectrum = forward(0)
    for p in range(5):
        corrected = correction(p, spectrum)
        ahead = forward(p + 1) if p < 4 else None
        returned = transform(left, right, corrected)
        gather(p, patches, returned)
        if ahead:
            patches, spectrum = ahead
    for e in range(energies):
        own_ref[e] = top_ref[e] - step[e] * total[e, :, :half]
        carried_ref[e] = step[e] * total[e, :, half:]


def band_update(chunk, own_cols, left, right, top, low, probe, measured):
    _, parts, rows, cols = top.shape
    _, modes, _, width, _ = probe.shape
    positions = measured.shape[1]
    start = chunk * CHUNK // GROUP
    band = pl.BlockSpec((GROUP, parts, rows, cols), lambda e: (e, 0, 0, 0))
    table = pl.BlockSpec(left.shape, lambda e: (0, 0))
    pairs = CHUNK * positions
    return pl.pallas_call(
        gradient_kernel,
        grid=(CHUNK // GROUP,),
        in_specs=[
            pl.BlockSpec(memory_space=pltpu.SMEM),
            table,
            table,
            pl.BlockSpec((GROUP, parts, rows, cols), lambda e: (e + start, 0, 0, 0)),
            band,
            pl.BlockSpec((GROUP, modes, parts, width, width), lambda e: (e + start, 0, 0, 0, 0)),
            pl.BlockSpec((GROUP, positions, width, width), lambda e: (e + start, 0, 0, 0)),
        ],
        out_specs=[band, band],
        out_shape=[jax.ShapeDtypeStruct((CHUNK, parts, rows, cols), jnp.float32)] * 2,
        scratch_shapes=[pltpu.VMEM((GROUP, parts, width, cols), jnp.float32)],
        cost_estimate=pl.CostEstimate(
            flops=pairs * 500_000_000, bytes_accessed=pairs * 200_000, transcendentals=0
        ),
        name="band_update",
    )(own_cols, left, right, top, low, probe, measured)


def spread(matrix):
    wide = jnp.kron(matrix, jnp.eye(SUBLANES, dtype=jnp.float32))
    high = lax.reduce_precision(wide, 8, 7)
    return jnp.concatenate(
        [jnp.concatenate([part, part], axis=1) for part in (high, wide - high)], axis=0
    ).astype(jnp.bfloat16)


def times(weight, values):
    high = values.astype(jnp.bfloat16)
    low = (values - high.astype(jnp.float32)).astype(jnp.bfloat16)
    products = jnp.dot(
        weight, jnp.concatenate([high, low], axis=0), preferred_element_type=jnp.float32
    )
    rows = products.shape[0] // 2
    return products[:rows] + products[rows:]


def project_kernel(place_ref, weight_ref, *refs):
    chunks = 2
    owns, received, outs = refs[:chunks], refs[chunks:2 * chunks], refs[2 * chunks:]
    energies, parts = owns[0].shape[:2]
    slots = len(outs)
    weight = weight_ref[...]
    for d in range(slots):
        at = lax.rem(place_ref[0] + d, slots)
        values = [
            own[e, q, at, 0] - got[e, q, at, 0]
            for own, got in zip(owns, received) for e in range(energies) for q in range(parts)
        ]
        outs[d][...] = times(weight, jnp.concatenate(values, axis=0))


def project(half, place, weight, owns, received):
    slots = 4
    chunk, parts, _, columns = owns[0].shape
    shape = (chunk, parts, slots, 2, SUBLANES, columns)
    block = pl.BlockSpec(shape[:3] + (1,) + shape[4:], lambda i: (0, 0, 0, half, 0, 0))
    arrays = [a.reshape(shape) for a in (*owns, *received)]
    out = jax.ShapeDtypeStruct((weight.shape[0] // 2, columns), jnp.float32)
    return pl.pallas_call(
        project_kernel,
        grid=(1,),
        in_specs=[
            pl.BlockSpec(memory_space=pltpu.SMEM), pl.BlockSpec(weight.shape, lambda i: (0, 0))
        ] + [block] * len(arrays),
        out_specs=[pl.BlockSpec(out.shape, lambda i: (0, 0))] * slots,
        out_shape=[out] * slots,
        cost_estimate=pl.CostEstimate(flops=400_000_000, bytes_accessed=2_000_000, transcendentals=0),
        name="project",
    )(place, weight, *arrays)


def expand_kernel(place_ref, weight_ref, *refs):
    slots = 4
    pieces, refined_ref = refs[:slots], refs[-1]
    parts = refined_ref.shape[1]
    weight = weight_ref[...]
    for d, piece in enumerate(pieces):
        values = times(weight, piece[...])
        at = lax.rem(place_ref[0] + slots - d, slots)
        for j in range(values.shape[0] // SUBLANES):
            refined_ref[j // parts, j % parts, at, 0] = values[j * SUBLANES:(j + 1) * SUBLANES]


def expand(half, place, weight, pieces, shape, previous):
    smem = pl.BlockSpec(memory_space=pltpu.SMEM)
    in_specs = [smem] + [pl.BlockSpec(a.shape, lambda i: (0, 0)) for a in (weight, *pieces)]
    aliases = {}
    if previous:
        aliases = {len(in_specs): 0}
        in_specs += [pl.BlockSpec(memory_space=pl.ANY)]
    return pl.pallas_call(
        expand_kernel,
        grid=(1,),
        in_specs=in_specs,
        out_specs=pl.BlockSpec(shape[:3] + (1,) + shape[4:], lambda i: (0, 0, 0, half, 0, 0)),
        out_shape=jax.ShapeDtypeStruct(shape, jnp.float32),
        input_output_aliases=aliases,
        cost_estimate=pl.CostEstimate(flops=400_000_000, bytes_accessed=2_000_000, transcendentals=0),
        name="expand",
    )(place, weight, *pieces, *previous)


def pick_kernel(place_ref, order_ref, first_ref, second_ref, out_ref):
    second = place_ref[1] == 1
    for m in range(out_ref.shape[0]):
        for q in range(out_ref.shape[1]):
            row = (order_ref[m] * out_ref.shape[1] + q) * SUBLANES
            at = pl.ds(pl.multiple_of(row, SUBLANES), SUBLANES)
            out_ref[m, q, 0] = jnp.where(second, second_ref[at], first_ref[at])


def pick(place, order, first, second, shape):
    smem = pl.BlockSpec(memory_space=pltpu.SMEM)
    vmem = pl.BlockSpec(memory_space=pltpu.VMEM)
    return pl.pallas_call(
        pick_kernel,
        in_specs=[smem, smem, vmem, vmem],
        out_specs=vmem,
        out_shape=jax.ShapeDtypeStruct(shape, jnp.float32),
        cost_estimate=pl.CostEstimate(flops=1_000_000, bytes_accessed=600_000, transcendentals=0),
        name="pick",
    )(place, order, first, second)


def build_basis(spectra):
    spectra_real = spectra[:, 0]
    spectra_imag = spectra[:, 1]
    upper_rows = jnp.stack([spectra_real, -spectra_imag], axis=-1)
    lower_rows = jnp.stack([spectra_imag, spectra_real], axis=-1)
    stacked = jnp.stack([upper_rows, lower_rows], axis=1)
    return stacked.reshape(2 * spectra.shape[0], 2 * spectra.shape[2])


def along_x(block, distance):
    return lax.ppermute(block, "energy", [(e, (e + 2 * distance) % 8) for e in range(8)])


def along_z(block):
    return lax.ppermute(block, "energy", [(e, e ^ 1) for e in range(8)])


def on_device(object_field, probe_modes, measured, scan_cols, spectra, material_order):
    energies, parts, _, columns = object_field.shape
    materials = spectra.shape[2]
    left, right = dft_tables(probe_modes.shape[-1])
    measured = measured[:, 0]
    own_cols = lax.dynamic_index_in_dim(scan_cols, lax.axis_index("strip"), 0, keepdims=False)
    lows = [
        shifted(object_field[e:e + CHUNK], "strip", -1) for e in range(0, energies, CHUNK)
    ]
    energy = lax.axis_index("energy")
    place = jnp.stack([energy // 2, energy % 2]).astype(jnp.int32)
    basis_matrix = build_basis(spectra)
    gram_matrix = jnp.dot(basis_matrix.T, basis_matrix, precision=PRECISE)
    factor = jnp.linalg.cholesky(gram_matrix)
    basis_own = lax.dynamic_slice_in_dim(
        basis_matrix, energy * energies * parts, energies * parts, axis=0
    )
    solver_own = jax.scipy.linalg.cho_solve((factor, True), basis_own.T)
    spread_solver, spread_basis = spread(solver_own), spread(basis_own)

    owns, received = [], []
    for chunk, low in enumerate(lows):
        own, carried = band_update(
            chunk, own_cols, left, right, object_field, low, probe_modes, measured
        )
        owns.append(own)
        received.append(shifted(carried, "strip", 1))
    mine = []
    for h in range(2):
        share, *others = project(h, place, spread_solver, owns, received)
        arrived = [along_x(other, d + 1) for d, other in enumerate(others)]
        share = share + arrived[0] + arrived[1] + arrived[2]
        arrived = along_z(share)
        mine.append(share + arrived)
    abundance = pick(
        place, material_order, *mine, (materials, parts, 1, SUBLANES, columns)
    )
    refined = ()
    shape = (energies, parts, 4, 2, SUBLANES, columns)
    for h in range(2):
        near = {d: along_x(mine[h], d) for d in (1, 3)}
        far = along_x(near[1 + 2 * h], 1 + 2 * h)
        pieces = [mine[h], near[1], far, near[3]]
        refined = (expand(h, place, spread_basis, pieces, shape, refined),)
    return refined[0].reshape(object_field.shape), abundance


def solution(mesh):
    return jax.shard_map(
        on_device,
        mesh=mesh,
        in_specs=(
            P("energy", None, "strip", None),
            P("energy", None, None, None, None),
            P("energy", "strip", None, None, None),
            P(),
            P(),
            P(),
        ),
        out_specs=(P("energy", None, "strip", None), P(None, None, "strip", "energy", None)),
        check_vma=False,
    )
```

```python
import functools

import jax
import jax.numpy as jnp
import numpy as np
from jax import lax
from jax.experimental import pallas as pl
from jax.experimental.pallas import tpu as pltpu
from jax.sharding import PartitionSpec as P


PRECISE = lax.Precision.HIGHEST
LANES = 128
SUBLANES = 8
GROUP = 2
CHUNK = 4


def shifted(block, axis, distance):
    devices = range(lax.axis_size(axis))
    route = [(i - distance, i) for i in devices if i - distance in devices]
    return lax.ppermute(block, axis, route)


def dft_tables(width):
    counter = np.arange(width)
    angle = 2.0 * np.pi * (counter[:, None] * counter[None, :] % width) / width
    cosine = (np.cos(angle) / np.sqrt(width)).astype(np.float32)
    sine = (np.sin(angle) / np.sqrt(width)).astype(np.float32)
    left = np.block([[cosine, sine], [-sine, cosine]])
    right = np.block([[cosine, -sine], [sine, cosine]])
    return jnp.asarray(left).astype(jnp.bfloat16), jnp.asarray(right).astype(jnp.bfloat16)


def transform(left, right, waves):
    width = waves[0][0].shape[0]
    stacked = jnp.concatenate([jnp.concatenate(pair, axis=0) for pair in waves], axis=1)
    half = jnp.dot(left, stacked, preferred_element_type=jnp.float32).astype(jnp.bfloat16)
    rows = []
    for m in range(len(waves)):
        cols = slice(m * width, (m + 1) * width)
        rows.append(jnp.concatenate([half[:width, cols], half[width:, cols]], axis=1))
    full = jnp.dot(
        jnp.concatenate(rows, axis=0), right, preferred_element_type=jnp.float32
    )
    return [
        (full[m * width:(m + 1) * width, :width], full[m * width:(m + 1) * width, width:])
        for m in range(len(waves))
    ]


def gradient_kernel(
    cols_ref, left_ref, right_ref, top_ref, low_ref, probe_ref, measured_ref,
    own_ref, carried_ref, total,
):
    energies, modes = probe_ref.shape[:2]
    width = probe_ref.shape[-1]
    half = width // 2
    left, right = left_ref[...], right_ref[...]
    lane = lax.broadcasted_iota(jnp.int32, (width, width), 1)
    power = [
        sum(probe_ref[e, m, q] * probe_ref[e, m, q] for m in range(modes) for q in range(2))
        for e in range(energies)
    ]
    step = [
        0.5 / jnp.max(jnp.max(p, axis=0, keepdims=True), axis=1, keepdims=True) for p in power
    ]

    def window(e, part, start):
        cols = pl.ds(start, LANES)
        return jnp.concatenate([top_ref[e, part, :, cols], low_ref[e, part, :, cols]], axis=0)

    bases = [0, 0, pl.multiple_of(cols_ref[2] // LANES * LANES, LANES), LANES, 2 * LANES]
    moves = [None, cols_ref[1], cols_ref[2] - bases[2], cols_ref[3] - LANES, None]

    def patch_of(e, p):
        base, offset = bases[p], moves[p]
        if offset is None:
            return [window(e, part, base) for part in range(2)]
        back = lax.rem(LANES - offset, LANES)
        patch = []
        for part in range(2):
            here = pltpu.roll(window(e, part, base), back, 1)
            there = pltpu.roll(window(e, part, base + LANES), back, 1)
            patch.append(jnp.where(lane < LANES - offset, here, there))
        return patch

    def add(e, part, start, value):
        at = pl.ds(start, LANES)
        total[e, part, :, at] += value

    def forward(p):
        waves, patches = [], [patch_of(e, p) for e in range(energies)]
        for e in range(energies):
            real, imag = patches[e]
            for m in range(modes):
                pr, pi = probe_ref[e, m, 0], probe_ref[e, m, 1]
                waves.append((
                    (pr * real - pi * imag).astype(jnp.bfloat16),
                    (pr * imag + pi * real).astype(jnp.bfloat16),
                ))
        return patches, transform(left, right, waves)

    def correction(p, spectrum):
        corrected = []
        for e in range(energies):
            mine = spectrum[e * modes:(e + 1) * modes]
            intensity = sum(r * r + i * i for r, i in mine)
            scale = measured_ref[e, p] * lax.rsqrt(jnp.maximum(intensity, 0.25))
            flipped = -scale
            corrected += [
                ((r * scale).astype(jnp.bfloat16), (i * flipped).astype(jnp.bfloat16))
                for r, i in mine
            ]
        return corrected

    def gather(p, patches, returned):
        for e in range(energies):
            patch = patches[e]
            grads = [power[e] * patch[0], power[e] * patch[1]]
            for m in range(modes):
                pr, pi = probe_ref[e, m, 0], probe_ref[e, m, 1]
                rr, ri = returned[e * modes + m]
                grads[0] -= pr * rr - pi * ri
                grads[1] += pr * ri + pi * rr
            for part, grad in enumerate(grads):
                if p == 0:
                    total[e, part, :, :LANES] = grad
                elif moves[p] is None:
                    add(e, part, bases[p], grad)
                else:
                    moved = pltpu.roll(grad, moves[p], 1)
                    add(e, part, bases[p], jnp.where(lane >= moves[p], moved, 0.0))
                    there = jnp.where(lane < moves[p], moved, 0.0)
                    if p == 1:
                        total[e, part, :, LANES:2 * LANES] = there
                        total[e, part, :, 2 * LANES:] = jnp.zeros((width, LANES), jnp.float32)
                    else:
                        add(e, part, bases[p] + LANES, there)

    patches, spectrum = forward(0)
    for p in range(5):
        corrected = correction(p, spectrum)
        ahead = forward(p + 1) if p < 4 else None
        returned = transform(left, right, corrected)
        gather(p, patches, returned)
        if ahead:
            patches, spectrum = ahead
    for e in range(energies):
        own_ref[e] = top_ref[e] - step[e] * total[e, :, :half]
        carried_ref[e] = step[e] * total[e, :, half:]


def band_update(chunk, own_cols, left, right, top, low, probe, measured):
    _, parts, rows, cols = top.shape
    _, modes, _, width, _ = probe.shape
    positions = measured.shape[1]
    start = chunk * CHUNK // GROUP
    band = pl.BlockSpec((GROUP, parts, rows, cols), lambda e: (e, 0, 0, 0))
    table = pl.BlockSpec(left.shape, lambda e: (0, 0))
    pairs = CHUNK * positions
    return pl.pallas_call(
        gradient_kernel,
        grid=(CHUNK // GROUP,),
        in_specs=[
            pl.BlockSpec(memory_space=pltpu.SMEM),
            table,
            table,
            pl.BlockSpec((GROUP, parts, rows, cols), lambda e: (e + start, 0, 0, 0)),
            band,
            pl.BlockSpec((GROUP, modes, parts, width, width), lambda e: (e + start, 0, 0, 0, 0)),
            pl.BlockSpec((GROUP, positions, width, width), lambda e: (e + start, 0, 0, 0)),
        ],
        out_specs=[band, band],
        out_shape=[jax.ShapeDtypeStruct((CHUNK, parts, rows, cols), jnp.float32)] * 2,
        scratch_shapes=[pltpu.VMEM((GROUP, parts, width, cols), jnp.float32)],
        cost_estimate=pl.CostEstimate(
            flops=pairs * 500_000_000, bytes_accessed=pairs * 200_000, transcendentals=0
        ),
        name="band_update",
    )(own_cols, left, right, top, low, probe, measured)


def spread(matrix):
    wide = jnp.kron(matrix, jnp.eye(SUBLANES, dtype=jnp.float32))
    high = lax.reduce_precision(wide, 8, 7)
    return jnp.concatenate(
        [jnp.concatenate([part, part], axis=1) for part in (high, wide - high)], axis=0
    ).astype(jnp.bfloat16)


def times(weight, values):
    high = values.astype(jnp.bfloat16)
    low = (values - high.astype(jnp.float32)).astype(jnp.bfloat16)
    products = jnp.dot(
        weight, jnp.concatenate([high, low], axis=0), preferred_element_type=jnp.float32
    )
    rows = products.shape[0] // 2
    return products[:rows] + products[rows:]


def project_kernel(half, place_ref, weight_ref, *refs):
    chunks, slots = 2, 4
    sources, outs = refs[:2 * chunks], refs[2 * chunks:2 * chunks + slots]
    taken, results, arrivals, departures = refs[2 * chunks + slots:]
    weight = weight_ref[...]
    loads = []
    for d in range(slots):
        at = lax.rem(place_ref[0] + d, slots)
        loads.append([
            pltpu.make_async_copy(a.at[:, :, at, half], taken.at[d, i], arrivals.at[d, i])
            for i, a in enumerate(sources)
        ])
        for load in loads[d]:
            load.start()
    stores = []
    for d in range(slots):
        for load in loads[d]:
            load.wait()
        values = [
            taken[d, i, e, q] - taken[d, chunks + i, e, q]
            for i in range(chunks)
            for e in range(taken.shape[2]) for q in range(taken.shape[3])
        ]
        results[d] = times(weight, jnp.concatenate(values, axis=0))
        stores.append(pltpu.make_async_copy(results.at[d], outs[d], departures.at[d]))
        stores[d].start()
    for store in stores:
        store.wait()


def project(half, place, weight, owns, received):
    slots = 4
    chunk, parts, _, columns = owns[0].shape
    shape = (chunk, parts, slots, 2, SUBLANES, columns)
    arrays = [a.reshape(shape) for a in (*owns, *received)]
    out = jax.ShapeDtypeStruct((weight.shape[0] // 2, columns), jnp.float32)
    return pl.pallas_call(
        functools.partial(project_kernel, half),
        in_specs=[
            pl.BlockSpec(memory_space=pltpu.SMEM), pl.BlockSpec(memory_space=pltpu.VMEM)
        ] + [pl.BlockSpec(memory_space=pl.ANY)] * len(arrays),
        out_specs=[pl.BlockSpec(memory_space=pl.ANY)] * slots,
        out_shape=[out] * slots,
        scratch_shapes=[
            pltpu.VMEM((slots, len(arrays), chunk, parts, SUBLANES, columns), jnp.float32),
            pltpu.VMEM((slots,) + out.shape, jnp.float32),
            pltpu.SemaphoreType.DMA((slots, len(arrays))),
            pltpu.SemaphoreType.DMA((slots,)),
        ],
        cost_estimate=pl.CostEstimate(flops=400_000_000, bytes_accessed=2_000_000, transcendentals=0),
        compiler_params=pltpu.CompilerParams(vmem_limit_bytes=67_000_000),
        name="project",
    )(place, weight, *arrays)


def expand_kernel(half, previous, place_ref, weight_ref, *refs):
    slots = 4
    pieces = refs[:slots]
    refined_ref, taken, results, arrivals, departures = refs[slots + previous:]
    parts = refined_ref.shape[1]
    weight = weight_ref[...]
    loads = [
        pltpu.make_async_copy(piece, taken.at[d], arrivals.at[d]) for d, piece in enumerate(pieces)
    ]
    for load in loads:
        load.start()
    stores = []
    for d in range(slots):
        loads[d].wait()
        values = times(weight, taken[d])
        for j in range(values.shape[0] // SUBLANES):
            results[d, j // parts, j % parts] = values[j * SUBLANES:(j + 1) * SUBLANES]
        at = lax.rem(place_ref[0] + slots - d, slots)
        stores.append(
            pltpu.make_async_copy(
                results.at[d], refined_ref.at[:, :, at, half], departures.at[d]
            )
        )
        stores[d].start()
    for store in stores:
        store.wait()


def expand(half, place, weight, pieces, shape, previous):
    slots = len(pieces)
    anywhere = pl.BlockSpec(memory_space=pl.ANY)
    in_specs = [pl.BlockSpec(memory_space=pltpu.SMEM), pl.BlockSpec(memory_space=pltpu.VMEM)]
    in_specs += [anywhere] * (slots + len(previous))
    return pl.pallas_call(
        functools.partial(expand_kernel, half, len(previous)),
        in_specs=in_specs,
        out_specs=anywhere,
        out_shape=jax.ShapeDtypeStruct(shape, jnp.float32),
        scratch_shapes=[
            pltpu.VMEM((slots,) + pieces[0].shape, jnp.float32),
            pltpu.VMEM((slots,) + shape[:2] + shape[4:], jnp.float32),
            pltpu.SemaphoreType.DMA((slots,)),
            pltpu.SemaphoreType.DMA((slots,)),
        ],
        input_output_aliases={2 + slots: 0} if previous else {},
        cost_estimate=pl.CostEstimate(flops=400_000_000, bytes_accessed=2_000_000, transcendentals=0),
        compiler_params=pltpu.CompilerParams(vmem_limit_bytes=67_000_000),
        name="expand",
    )(place, weight, *pieces, *previous)


def pick_kernel(place_ref, order_ref, first_ref, second_ref, out_ref):
    second = place_ref[1] == 1
    for m in range(out_ref.shape[0]):
        for q in range(out_ref.shape[1]):
            row = (order_ref[m] * out_ref.shape[1] + q) * SUBLANES
            at = pl.ds(pl.multiple_of(row, SUBLANES), SUBLANES)
            out_ref[m, q, 0] = jnp.where(second, second_ref[at], first_ref[at])


def pick(place, order, first, second, shape):
    smem = pl.BlockSpec(memory_space=pltpu.SMEM)
    vmem = pl.BlockSpec(memory_space=pltpu.VMEM)
    return pl.pallas_call(
        pick_kernel,
        in_specs=[smem, smem, vmem, vmem],
        out_specs=vmem,
        out_shape=jax.ShapeDtypeStruct(shape, jnp.float32),
        cost_estimate=pl.CostEstimate(flops=1_000_000, bytes_accessed=600_000, transcendentals=0),
        name="pick",
    )(place, order, first, second)


def build_basis(spectra):
    spectra_real = spectra[:, 0]
    spectra_imag = spectra[:, 1]
    upper_rows = jnp.stack([spectra_real, -spectra_imag], axis=-1)
    lower_rows = jnp.stack([spectra_imag, spectra_real], axis=-1)
    stacked = jnp.stack([upper_rows, lower_rows], axis=1)
    return stacked.reshape(2 * spectra.shape[0], 2 * spectra.shape[2])


def along_x(block, distance):
    return lax.ppermute(block, "energy", [(e, (e + 2 * distance) % 8) for e in range(8)])


def along_z(block):
    return lax.ppermute(block, "energy", [(e, e ^ 1) for e in range(8)])


def on_device(object_field, probe_modes, measured, scan_cols, spectra, material_order):
    energies, parts, _, columns = object_field.shape
    materials = spectra.shape[2]
    left, right = dft_tables(probe_modes.shape[-1])
    measured = measured[:, 0]
    own_cols = lax.dynamic_index_in_dim(scan_cols, lax.axis_index("strip"), 0, keepdims=False)
    lows = [
        shifted(object_field[e:e + CHUNK], "strip", -1) for e in range(0, energies, CHUNK)
    ]
    energy = lax.axis_index("energy")
    place = jnp.stack([energy // 2, energy % 2]).astype(jnp.int32)
    basis_matrix = build_basis(spectra)
    gram_matrix = jnp.dot(basis_matrix.T, basis_matrix, precision=PRECISE)
    factor = jnp.linalg.cholesky(gram_matrix)
    basis_own = lax.dynamic_slice_in_dim(
        basis_matrix, energy * energies * parts, energies * parts, axis=0
    )
    solver_own = jax.scipy.linalg.cho_solve((factor, True), basis_own.T)
    spread_solver, spread_basis = spread(solver_own), spread(basis_own)

    owns, received = [], []
    for chunk, low in enumerate(lows):
        own, carried = band_update(
            chunk, own_cols, left, right, object_field, low, probe_modes, measured
        )
        owns.append(own)
        received.append(shifted(carried, "strip", 1))
    mine = []
    for h in range(2):
        share, *others = project(h, place, spread_solver, owns, received)
        arrived = [along_x(other, d + 1) for d, other in enumerate(others)]
        share = share + arrived[0] + arrived[1] + arrived[2]
        arrived = along_z(share)
        mine.append(share + arrived)
    abundance = pick(
        place, material_order, *mine, (materials, parts, 1, SUBLANES, columns)
    )
    refined = ()
    shape = (energies, parts, 4, 2, SUBLANES, columns)
    for h in range(2):
        pieces = [mine[h]] + [along_x(mine[h], d) for d in (1, 2, 3)]
        refined = (expand(h, place, spread_basis, pieces, shape, refined),)
    return refined[0].reshape(object_field.shape), abundance


def solution(mesh):
    return jax.shard_map(
        on_device,
        mesh=mesh,
        in_specs=(
            P("energy", None, "strip", None),
            P("energy", None, None, None, None),
            P("energy", "strip", None, None, None),
            P(),
            P(),
            P(),
        ),
        out_specs=(P("energy", None, "strip", None), P(None, None, "strip", "energy", None)),
        check_vma=False,
    )
```

```python
import jax
import jax.numpy as jnp
import numpy as np
from jax import lax
from jax.experimental import pallas as pl
from jax.experimental.pallas import tpu as pltpu
from jax.sharding import PartitionSpec as P


PRECISE = lax.Precision.HIGHEST
LANES = 128
SUBLANES = 8
GROUP = 2
CHUNK = 4


def shifted(block, axis, distance):
    devices = range(lax.axis_size(axis))
    route = [(i - distance, i) for i in devices if i - distance in devices]
    return lax.ppermute(block, axis, route)


def dft_tables(width):
    counter = np.arange(width)
    angle = 2.0 * np.pi * (counter[:, None] * counter[None, :] % width) / width
    cosine = (np.cos(angle) / np.sqrt(width)).astype(np.float32)
    sine = (np.sin(angle) / np.sqrt(width)).astype(np.float32)
    left = np.block([[cosine, sine], [-sine, cosine]])
    right = np.block([[cosine, -sine], [sine, cosine]])
    return jnp.asarray(left).astype(jnp.bfloat16), jnp.asarray(right).astype(jnp.bfloat16)


def transform(left, right, waves):
    width = waves[0][0].shape[0]
    stacked = jnp.concatenate([jnp.concatenate(pair, axis=0) for pair in waves], axis=1)
    half = jnp.dot(left, stacked, preferred_element_type=jnp.float32).astype(jnp.bfloat16)
    rows = []
    for m in range(len(waves)):
        cols = slice(m * width, (m + 1) * width)
        rows.append(jnp.concatenate([half[:width, cols], half[width:, cols]], axis=1))
    full = jnp.dot(
        jnp.concatenate(rows, axis=0), right, preferred_element_type=jnp.float32
    )
    return [
        (full[m * width:(m + 1) * width, :width], full[m * width:(m + 1) * width, width:])
        for m in range(len(waves))
    ]


def gradient_kernel(
    cols_ref, left_ref, right_ref, top_ref, low_ref, probe_ref, measured_ref,
    own_ref, *refs,
):
    energies, modes = probe_ref.shape[:2]
    width = probe_ref.shape[-1]
    half = width // 2
    *carried_refs, total = refs
    left, right = left_ref[...], right_ref[...]
    lane = lax.broadcasted_iota(jnp.int32, (width, width), 1)
    power = [
        sum(probe_ref[e, m, q] * probe_ref[e, m, q] for m in range(modes) for q in range(2))
        for e in range(energies)
    ]
    step = [
        0.5 / jnp.max(jnp.max(p, axis=0, keepdims=True), axis=1, keepdims=True) for p in power
    ]

    def window(e, part, start):
        cols = pl.ds(start, LANES)
        return jnp.concatenate([top_ref[e, part, :, cols], low_ref[e, part, :, cols]], axis=0)

    bases = [0, 0, pl.multiple_of(cols_ref[2] // LANES * LANES, LANES), LANES, 2 * LANES]
    moves = [None, cols_ref[1], cols_ref[2] - bases[2], cols_ref[3] - LANES, None]

    def patch_of(e, p):
        base, offset = bases[p], moves[p]
        if offset is None:
            return [window(e, part, base) for part in range(2)]
        back = lax.rem(LANES - offset, LANES)
        patch = []
        for part in range(2):
            here = pltpu.roll(window(e, part, base), back, 1)
            there = pltpu.roll(window(e, part, base + LANES), back, 1)
            patch.append(jnp.where(lane < LANES - offset, here, there))
        return patch

    def add(e, part, start, value):
        at = pl.ds(start, LANES)
        total[e, part, :, at] += value

    def forward(p):
        waves, patches = [], [patch_of(e, p) for e in range(energies)]
        for e in range(energies):
            real, imag = patches[e]
            for m in range(modes):
                pr, pi = probe_ref[e, m, 0], probe_ref[e, m, 1]
                waves.append((
                    (pr * real - pi * imag).astype(jnp.bfloat16),
                    (pr * imag + pi * real).astype(jnp.bfloat16),
                ))
        return patches, transform(left, right, waves)

    def correction(p, spectrum):
        corrected = []
        for e in range(energies):
            mine = spectrum[e * modes:(e + 1) * modes]
            intensity = sum(r * r + i * i for r, i in mine)
            scale = measured_ref[e, p] * lax.rsqrt(jnp.maximum(intensity, 0.25))
            flipped = -scale
            corrected += [
                ((r * scale).astype(jnp.bfloat16), (i * flipped).astype(jnp.bfloat16))
                for r, i in mine
            ]
        return corrected

    def gather(p, patches, returned):
        for e in range(energies):
            patch = patches[e]
            grads = [power[e] * patch[0], power[e] * patch[1]]
            for m in range(modes):
                pr, pi = probe_ref[e, m, 0], probe_ref[e, m, 1]
                rr, ri = returned[e * modes + m]
                grads[0] -= pr * rr - pi * ri
                grads[1] += pr * ri + pi * rr
            for part, grad in enumerate(grads):
                if p == 0:
                    total[e, part, :, :LANES] = grad
                elif moves[p] is None:
                    add(e, part, bases[p], grad)
                else:
                    moved = pltpu.roll(grad, moves[p], 1)
                    add(e, part, bases[p], jnp.where(lane >= moves[p], moved, 0.0))
                    there = jnp.where(lane < moves[p], moved, 0.0)
                    if p == 1:
                        total[e, part, :, LANES:2 * LANES] = there
                        total[e, part, :, 2 * LANES:] = jnp.zeros((width, LANES), jnp.float32)
                    else:
                        add(e, part, bases[p] + LANES, there)

    patches, spectrum = forward(0)
    for p in range(5):
        corrected = correction(p, spectrum)
        ahead = forward(p + 1) if p < 4 else None
        returned = transform(left, right, corrected)
        gather(p, patches, returned)
        if ahead:
            patches, spectrum = ahead
    for e in range(energies):
        own_ref[e] = top_ref[e] - step[e] * total[e, :, :half]
        if len(carried_refs) == 1:
            carried_refs[0][e] = step[e] * total[e, :, half:]
        else:
            for group in range(half // SUBLANES):
                at = slice(half + group * SUBLANES, half + (group + 1) * SUBLANES)
                carried_refs[group % 2][e, :, group // 2, 0] = step[e] * total[e, :, at]


def band_update(chunk, own_cols, left, right, top, low, probe, measured):
    _, parts, rows, cols = top.shape
    _, modes, _, width, _ = probe.shape
    positions = measured.shape[1]
    start = chunk * CHUNK // GROUP
    band = pl.BlockSpec((GROUP, parts, rows, cols), lambda e: (e, 0, 0, 0))
    table = pl.BlockSpec(left.shape, lambda e: (0, 0))
    pairs = CHUNK * positions
    if chunk == 0:
        carried, carried_shapes = band, [(CHUNK, parts, rows, cols)]
    else:
        tail = (parts, rows // (2 * SUBLANES), 1, SUBLANES, cols)
        carried = pl.BlockSpec((GROUP,) + tail, lambda e: (e, 0, 0, 0, 0, 0))
        carried_shapes = [(CHUNK,) + tail] * 2
    return pl.pallas_call(
        gradient_kernel,
        grid=(CHUNK // GROUP,),
        in_specs=[
            pl.BlockSpec(memory_space=pltpu.SMEM),
            table,
            table,
            pl.BlockSpec((GROUP, parts, rows, cols), lambda e: (e + start, 0, 0, 0)),
            band,
            pl.BlockSpec((GROUP, modes, parts, width, width), lambda e: (e + start, 0, 0, 0, 0)),
            pl.BlockSpec((GROUP, positions, width, width), lambda e: (e + start, 0, 0, 0)),
        ],
        out_specs=[band] + [carried] * len(carried_shapes),
        out_shape=[
            jax.ShapeDtypeStruct(shape, jnp.float32)
            for shape in [(CHUNK, parts, rows, cols)] + carried_shapes
        ],
        scratch_shapes=[pltpu.VMEM((GROUP, parts, width, cols), jnp.float32)],
        cost_estimate=pl.CostEstimate(
            flops=pairs * 500_000_000, bytes_accessed=pairs * 200_000, transcendentals=0
        ),
        name="band_update",
    )(own_cols, left, right, top, low, probe, measured)


def spread(matrix):
    wide = jnp.kron(matrix, jnp.eye(SUBLANES, dtype=jnp.float32))
    high = lax.reduce_precision(wide, 8, 7)
    return jnp.concatenate(
        [jnp.concatenate([part, part], axis=1) for part in (high, wide - high)], axis=0
    ).astype(jnp.bfloat16)


def times(weight, values):
    high = values.astype(jnp.bfloat16)
    low = (values - high.astype(jnp.float32)).astype(jnp.bfloat16)
    products = jnp.dot(
        weight, jnp.concatenate([high, low], axis=0), preferred_element_type=jnp.float32
    )
    rows = products.shape[0] // 2
    return products[:rows] + products[rows:]


def project_kernel(place_ref, weight_ref, *refs):
    chunks = 2
    owns, received, outs = refs[:chunks], refs[chunks:2 * chunks], refs[2 * chunks:]
    energies, parts = owns[0].shape[:2]
    slots = len(outs)
    weight = weight_ref[...]
    for d in range(slots):
        at = lax.rem(place_ref[0] + d, slots)
        values = [
            own[e, q, at, 0] - got[e, q, at, 0]
            for own, got in zip(owns, received) for e in range(energies) for q in range(parts)
        ]
        outs[d][...] = times(weight, jnp.concatenate(values, axis=0))


def project(half, place, weight, owns, received):
    slots = 4
    chunk, parts, _, columns = owns[0].shape
    shape = (chunk, parts, slots, 2, SUBLANES, columns)
    size = shape[:3] + (1,) + shape[4:]
    block = pl.BlockSpec(size, lambda i: (0, 0, 0, half, 0, 0))
    alone = pl.BlockSpec(size, lambda i: (0,) * 6)
    arrays = [a if a.shape == size else a.reshape(shape) for a in (*owns, *received)]
    out = jax.ShapeDtypeStruct((weight.shape[0] // 2, columns), jnp.float32)
    return pl.pallas_call(
        project_kernel,
        grid=(1,),
        in_specs=[
            pl.BlockSpec(memory_space=pltpu.SMEM), pl.BlockSpec(weight.shape, lambda i: (0, 0))
        ] + [alone if a.shape == size else block for a in arrays],
        out_specs=[pl.BlockSpec(out.shape, lambda i: (0, 0))] * slots,
        out_shape=[out] * slots,
        cost_estimate=pl.CostEstimate(flops=400_000_000, bytes_accessed=2_000_000, transcendentals=0),
        name="project",
    )(place, weight, *arrays)


def expand_kernel(place_ref, weight_ref, *refs):
    slots = 4
    pieces, refined_ref = refs[:slots], refs[-1]
    parts = refined_ref.shape[1]
    weight = weight_ref[...]
    for d, piece in enumerate(pieces):
        values = times(weight, piece[...])
        at = lax.rem(place_ref[0] + slots - d, slots)
        for j in range(values.shape[0] // SUBLANES):
            refined_ref[j // parts, j % parts, at, 0] = values[j * SUBLANES:(j + 1) * SUBLANES]


def expand(half, place, weight, pieces, shape, previous):
    smem = pl.BlockSpec(memory_space=pltpu.SMEM)
    in_specs = [smem] + [pl.BlockSpec(a.shape, lambda i: (0, 0)) for a in (weight, *pieces)]
    aliases = {}
    if previous:
        aliases = {len(in_specs): 0}
        in_specs += [pl.BlockSpec(memory_space=pl.ANY)]
    return pl.pallas_call(
        expand_kernel,
        grid=(1,),
        in_specs=in_specs,
        out_specs=pl.BlockSpec(shape[:3] + (1,) + shape[4:], lambda i: (0, 0, 0, half, 0, 0)),
        out_shape=jax.ShapeDtypeStruct(shape, jnp.float32),
        input_output_aliases=aliases,
        cost_estimate=pl.CostEstimate(flops=400_000_000, bytes_accessed=2_000_000, transcendentals=0),
        name="expand",
    )(place, weight, *pieces, *previous)


def pick_kernel(place_ref, order_ref, first_ref, second_ref, out_ref):
    second = place_ref[1] == 1
    for m in range(out_ref.shape[0]):
        for q in range(out_ref.shape[1]):
            row = (order_ref[m] * out_ref.shape[1] + q) * SUBLANES
            at = pl.ds(pl.multiple_of(row, SUBLANES), SUBLANES)
            out_ref[m, q, 0] = jnp.where(second, second_ref[at], first_ref[at])


def pick(place, order, first, second, shape):
    smem = pl.BlockSpec(memory_space=pltpu.SMEM)
    vmem = pl.BlockSpec(memory_space=pltpu.VMEM)
    return pl.pallas_call(
        pick_kernel,
        in_specs=[smem, smem, vmem, vmem],
        out_specs=vmem,
        out_shape=jax.ShapeDtypeStruct(shape, jnp.float32),
        cost_estimate=pl.CostEstimate(flops=1_000_000, bytes_accessed=600_000, transcendentals=0),
        name="pick",
    )(place, order, first, second)


def build_basis(spectra):
    spectra_real = spectra[:, 0]
    spectra_imag = spectra[:, 1]
    upper_rows = jnp.stack([spectra_real, -spectra_imag], axis=-1)
    lower_rows = jnp.stack([spectra_imag, spectra_real], axis=-1)
    stacked = jnp.stack([upper_rows, lower_rows], axis=1)
    return stacked.reshape(2 * spectra.shape[0], 2 * spectra.shape[2])


def along_x(block, distance):
    return lax.ppermute(block, "energy", [(e, (e + 2 * distance) % 8) for e in range(8)])


def along_z(block):
    return lax.ppermute(block, "energy", [(e, e ^ 1) for e in range(8)])


def on_device(object_field, probe_modes, measured, scan_cols, spectra, material_order):
    energies, parts, _, columns = object_field.shape
    materials = spectra.shape[2]
    left, right = dft_tables(probe_modes.shape[-1])
    measured = measured[:, 0]
    own_cols = lax.dynamic_index_in_dim(scan_cols, lax.axis_index("strip"), 0, keepdims=False)
    lows = [
        shifted(object_field[e:e + CHUNK], "strip", -1) for e in range(0, energies, CHUNK)
    ]
    energy = lax.axis_index("energy")
    place = jnp.stack([energy // 2, energy % 2]).astype(jnp.int32)
    basis_matrix = build_basis(spectra)
    gram_matrix = jnp.dot(basis_matrix.T, basis_matrix, precision=PRECISE)
    factor = jnp.linalg.cholesky(gram_matrix)
    basis_own = lax.dynamic_slice_in_dim(
        basis_matrix, energy * energies * parts, energies * parts, axis=0
    )
    solver_own = jax.scipy.linalg.cho_solve((factor, True), basis_own.T)
    spread_solver, spread_basis = spread(solver_own), spread(basis_own)

    owns, received = [], []
    for chunk, low in enumerate(lows):
        own, *carried = band_update(
            chunk, own_cols, left, right, object_field, low, probe_modes, measured
        )
        owns.append(own)
        received.append([shifted(block, "strip", 1) for block in carried])
    mine = []
    for h in range(2):
        share, *others = project(
            h, place, spread_solver, owns, [blocks[h % len(blocks)] for blocks in received]
        )
        arrived = [along_x(other, d + 1) for d, other in enumerate(others)]
        share = share + arrived[0] + arrived[1] + arrived[2]
        arrived = along_z(share)
        mine.append(share + arrived)
    abundance = pick(
        place, material_order, *mine, (materials, parts, 1, SUBLANES, columns)
    )
    refined = ()
    shape = (energies, parts, 4, 2, SUBLANES, columns)
    for h in range(2):
        pieces = [mine[h]] + [along_x(mine[h], d) for d in (1, 2, 3)]
        refined = (expand(h, place, spread_basis, pieces, shape, refined),)
    return refined[0].reshape(object_field.shape), abundance


def solution(mesh):
    return jax.shard_map(
        on_device,
        mesh=mesh,
        in_specs=(
            P("energy", None, "strip", None),
            P("energy", None, None, None, None),
            P("energy", "strip", None, None, None),
            P(),
            P(),
            P(),
        ),
        out_specs=(P("energy", None, "strip", None), P(None, None, "strip", "energy", None)),
        check_vma=False,
    )
```
